32 devices in a mesh: feat: 8 (over z, core), node: 4 (over y, x).
Axes of the slice: x: 2, y: 2, z: 4, core: 2. Of those that a mesh axis runs over, the one named last changes fastest.
Arguments:
- node_features: bfloat16 [1024, 4, 1024], P('feat', 'node'), may hold values from -6 to 6
- weight: bfloat16 [1024, 256], P('feat'), may hold values from -0.1875 to 0.1875
- out_bias: float32 [256], replicated, may hold values from -3 to 3
- edge_tiles: bfloat16 [4, 8, 8, 128, 128], P('node', 'feat'), may hold values from 0.049804688 to 1
- tile_column: int32 [4, 8, 8], P('node', 'feat'), may hold values from 0 to 7, as said below
- tile_count: int32 [4, 8], P('node', 'feat'), may hold values from 1 to 8, as said below
- grad_hidden: bfloat16 [4, 1024, 256], P('node', 'feat'), may hold values from -6 to 6
Outputs:
- hidden: bfloat16 [4, 1024, 256], P('node', 'feat')
- grad_features: bfloat16 [1024, 4, 1024], P('feat', 'node')
- weight_grad: float32 [1024, 256], P('feat')
The draws below stay inside these ranges and needn't reach their ends.
Inputs may be any that keep to these rules, and one draw needn't show every extreme that they name: `tile_column`: the 8 column blocks listed for one row block are distinct, live slots or not. `tile_count`: slots of a row block beyond its count are ignored. In every cluster some row block has exactly 8 live tiles.
All inputs are finite; a program needn't handle non-finite values.
Results may differ from the reference program's by a relative error of at most 0.007.
Values may be sent and summed in bfloat16 or wider, within the bound.
A program may use at most 64 MiB of HBM per device.

```python
import math
import jax
import jax.numpy as jnp
from jax import lax

F = 1024
H = 256
TILE = 128
TPR = 8
NBLK = 8
R = 1024
CLUSTERS = 4
NODES = 4096


def draw_tile_column(key, part):
    row_keys = jax.random.split(key, CLUSTERS * NBLK)

    def one_row(row_key):
        return jax.random.permutation(row_key, NBLK)[:TPR].astype(jnp.int32)
    picked = jax.vmap(one_row)(row_keys)
    return picked.reshape(CLUSTERS, NBLK, TPR)


def draw_tile_count(key, part):
    key_one, key_two, key_three = jax.random.split(key, 3)
    grid_shape = (CLUSTERS, NBLK)
    largest = jnp.maximum(jax.random.randint(key_one, grid_shape, 1, TPR + 1), jax.random.randint(key_two, grid_shape, 1, TPR + 1))
    busiest = jax.random.randint(key_three, (CLUSTERS, 1), 0, NBLK)
    block_ids = jnp.arange(NBLK, dtype=jnp.int32)[None, :]
    return jnp.where(block_ids == busiest, TPR, largest).astype(jnp.int32)


def block_scale(stream_key, dims, cuts, least, top_value):
    def one(axis_at, shards_of):
        heights = jax.random.uniform(jax.random.fold_in(jax.random.fold_in(stream_key, 6), axis_at), (shards_of,), jnp.float32, least / len(cuts), top_value / len(cuts))
        return jnp.repeat(jnp.exp(heights), dims[axis_at] // shards_of).reshape((-1,) + (1,) * (len(dims) - axis_at - 1))

    level = one(*cuts[0])
    for cut in cuts[1:]:
        level = level * one(*cut)
    return level


def centred(key, dims, width, reach, shards=(), kind=jnp.bfloat16):
    drawn = jax.random.normal(key, dims, jnp.float32) * width
    if len(shards) > 0:
        drawn = block_scale(key, dims, shards, -0.22, 0.18) * drawn
    return jnp.clip(drawn, min=-reach, max=reach).astype(kind)


def setup_inputs(seed: int = 0) -> dict:
    seeds = jax.random.split(jax.random.key(seed), 8)
    node_features = centred(seeds[0], (F, CLUSTERS, R), 1.0, 6.0, ((0, 8), (1, 4)))
    weight = centred(seeds[1], (F, H), F ** -0.5, 0.1875, ((0, 8),))
    out_bias = centred(seeds[2], (H,), 0.5, 3.0, (), jnp.float32)
    edge_tiles = jnp.clip(jnp.exp(math.log(1.0) - 2.9996462 * jax.random.uniform(seeds[3], (CLUSTERS, NBLK, TPR, TILE, TILE), jnp.float32) ** block_scale(seeds[3], (CLUSTERS, NBLK, TPR, TILE, TILE), ((0, 4), (1, 8)), -0.2, 0.2)), 0.049804688, 1.0).astype(jnp.bfloat16)
    tile_column = draw_tile_column(jax.random.fold_in(seeds[7], 71), 0)
    tile_count = draw_tile_count(jax.random.fold_in(seeds[7], 71), 0)
    grad_hidden = centred(seeds[6], (CLUSTERS, R, H), 1.0, 6.0, ((0, 4), (1, 8)))
    return {"node_features": node_features, "weight": weight, "out_bias": out_bias, "edge_tiles": edge_tiles, "tile_column": tile_column, "tile_count": tile_count, "grad_hidden": grad_hidden}


def gelu_tanh(pre_value):
    return jax.nn.gelu(pre_value, approximate=True)

def one_cluster(weight, out_bias, cluster_feats, cluster_tiles, cluster_cols, cluster_count, cluster_grad):
    slot_ids = jnp.arange(TPR, dtype=jnp.int32)
    projected = lax.dot_general(cluster_feats, weight, (((0,), (0,)), ((), ())), preferred_element_type=jnp.float32).astype(jnp.bfloat16)
    block_rows = projected.reshape(NBLK, TILE, H)
    live_mask = (slot_ids[None, :] < cluster_count[:, None]).astype(jnp.bfloat16)
    masked = cluster_tiles * live_mask[:, :, None, None]
    masked_wide = masked.astype(jnp.float32)
    degree = lax.optimization_barrier(jnp.sum(masked_wide, axis=(1, 3)))
    chosen = block_rows[cluster_cols]
    summed = jnp.einsum('bsij,bsjh->bih', masked_wide, chosen.astype(jnp.float32))
    row_scale = lax.rsqrt(degree)[:, :, None]
    pre_act = summed * row_scale + out_bias
    activated, backward = jax.vjp(gelu_tanh, pre_act)
    grad_pre, = backward(cluster_grad.reshape(NBLK, TILE, H).astype(jnp.float32))
    scaled = (grad_pre * row_scale).astype(jnp.bfloat16)
    tile_terms = jnp.einsum('bsij,bih->bsjh', masked_wide, scaled.astype(jnp.float32)).astype(jnp.bfloat16)
    grad_proj = jnp.zeros((NBLK, TILE, H), jnp.float32).at[cluster_cols].add(tile_terms.astype(jnp.float32))
    grad_rounded = grad_proj.astype(jnp.bfloat16).reshape(NBLK * TILE, H)
    grad_feat = lax.dot_general(weight, grad_rounded, (((1,), (1,)), ((), ())), preferred_element_type=jnp.float32).astype(jnp.bfloat16)
    grad_weight = lax.dot_general(cluster_feats, grad_rounded, (((1,), (0,)), ((), ())), preferred_element_type=jnp.float32)
    return (activated.astype(jnp.bfloat16).reshape(NBLK * TILE, H), grad_feat, grad_weight)

def reference(node_features, weight, out_bias, edge_tiles, tile_column, tile_count, grad_hidden):
    per_cluster = (jnp.moveaxis(node_features, 1, 0), edge_tiles, tile_column, tile_count, grad_hidden)

    def step_one(running, pieces):
        cluster_feats, cluster_tiles, cluster_cols, cluster_count, cluster_grad = pieces
        activated, grad_feat, grad_weight = one_cluster(weight, out_bias, cluster_feats, cluster_tiles, cluster_cols, cluster_count, cluster_grad)
        return (running + grad_weight, (activated, grad_feat))
    start_grad = jnp.zeros((F, H), jnp.float32)
    total_grad, (hidden, grad_cols) = lax.scan(step_one, start_grad, per_cluster)
    grad_features = jnp.moveaxis(grad_cols, 0, 1)
    weight_grad = total_grad * (1.0 / math.sqrt(NODES))
    return (hidden, grad_features, weight_grad)
```

```python
import functools
import math

import jax
import jax.numpy as jnp
from jax import lax
from jax.experimental import pallas as pl
from jax.experimental.pallas import tpu as pltpu
from jax.sharding import PartitionSpec as P

MESH = pl.DeviceIdType.MESH
F32 = jnp.float32
BF16 = jnp.bfloat16
CHUNKS = 2
EARLY = False
ROOT = math.sqrt(2.0 / math.pi)


def flip(index, bit):
    return index + bit * (1 - 2 * ((index // bit) % 2))


def flip_many(index, mask, steps):
    for j in range(steps):
        if (mask >> j) & 1:
            index = flip(index, 1 << j)
    return index


def tn(a, b):
    return lax.dot_general(a, b, (((0,), (0,)), ((), ())), preferred_element_type=F32)


def nt(a, b):
    return lax.dot_general(a, b, (((1,), (1,)), ((), ())), preferred_element_type=F32)


def nn(a, b):
    return lax.dot_general(a, b, (((1,), (0,)), ((), ())), preferred_element_type=F32)


def landed(ref, sem):
    pltpu.make_async_copy(ref, ref, sem).wait()


def kernel(sizes, cols_hbm, count_hbm, feats, weight_hbm, bias_hbm, tiles_hbm, grad_hbm,
           hidden, grad_feat, weight_grad,
           cols, count, weight, bias, tiles, grads,
           x_send, x_pair, w_pair, a_full, rs_out, rs_in, gath, sc_full, rt_out, rt_in,
           ggath, wg_in,
           small_s, xa_s, xb_s, sent_s, ex_r, x_r, rs_r, ag_r, fa_r, rt_r, gg_r, fw_r, wg_r,
           far, aside):
    zs, nodes, slots, tr, fd, hw, total = sizes
    zbits, nbits = zs.bit_length() - 1, nodes.bit_length() - 1
    hc = hw // CHUNKS
    ks = range(CHUNKS)
    feat_at = lax.axis_index("feat")
    node_at = lax.axis_index("node")
    core = feat_at % 2
    z = feat_at // 2
    mate = {"feat": z * 2 + 1 - core}
    line = zs == 4
    square = nodes == 4
    inner = jnp.logical_or(z == 1, z == 2)
    outer = jnp.logical_not(inner)

    zrel = [flip_many(z, r, zbits) for r in range(zs)]

    def z_peer(r):
        return {"feat": zrel[r] * 2 + core}

    def n_peer(n):
        return {"node": flip_many(node_at, n, nbits)}

    def push(src, dst, ss, rr, dev):
        pltpu.make_async_remote_copy(
            src_ref=src, dst_ref=dst, send_sem=ss, recv_sem=rr,
            device_id=dev, device_id_type=MESH).start()

    def signal(sem, dev):
        pl.semaphore_signal(sem, inc=1, device_id=dev, device_id_type=MESH)

    barrier = pltpu.get_barrier_semaphore()
    near_n = [1, 2] if square else list(range(1, nodes))
    near_z = [1] if line else list(range(1, zs))
    for r in near_z:
        signal(barrier, z_peer(r))
    if line:
        @pl.when(inner)
        def _():
            signal(barrier, z_peer(3))
    for n in near_n:
        signal(barrier, n_peer(n))
    signal(barrier, mate)

    def rows_of(r, parity):
        return pl.multiple_of((zrel[r] * 2 + parity) * tr, tr)

    def fetch(src, dst, sem):
        copy = pltpu.make_async_copy(src, dst, sem)
        copy.start()
        return copy

    order = list(reversed(range(1, zs)))
    loads = [fetch(src, dst, small_s.at[i]) for i, (src, dst) in enumerate((
        (weight_hbm, weight), (cols_hbm, cols), (count_hbm, count), (tiles_hbm, tiles),
        (bias_hbm, bias), (grad_hbm, grads.at[pl.ds(0, tr)])))]
    for r in range(zs):
        fetch(feats.at[:, pl.ds(rows_of(r, core), tr)], x_pair.at[r, pl.ds(0, fd)], xa_s)
    for r in range(zs):
        fetch(feats.at[:, pl.ds(rows_of(r, 1 - core), tr)], x_send.at[r], xb_s)
    loads[0].wait()
    w_pair[0:fd, :] = weight[...]
    for i in range(1, 4):
        loads[i].wait()
    live = count[0, 0]

    def listed(block):
        where = jnp.int32(0)
        alive = jnp.int32(0)
        for s in range(slots):
            hit = cols[0, 0, s] == block
            where = jnp.where(hit, s, where)
            alive = jnp.where(hit, jnp.where(s < live, 1, 0), alive)
        return tiles[where] * alive.astype(BF16)

    half = zs * tr

    def mask_tiles():
        for p in range(2):
            for r in range(zs):
                parity = core if p == 0 else 1 - core
                at = p * half + r * tr
                a_full[0:tr, at:at + tr] = listed(zrel[r] * 2 + parity)

    if EARLY:
        mask_tiles()
    landed(x_pair.at[:, pl.ds(0, fd)], xa_s)
    landed(x_send, xb_s)

    greeted = 1 + len(near_n) + len(near_z)
    if line:
        greeted = greeted + jnp.where(inner, 1, 0)
    pl.semaphore_wait(barrier, greeted)
    push(weight, w_pair.at[pl.ds(fd, fd)], sent_s.at[0], ex_r.at[0], mate)
    for r in order + [0]:
        push(x_send.at[r], x_pair.at[r, pl.ds(fd, fd)], sent_s.at[1], x_r.at[r], mate)
    if square:
        signal(aside, n_peer(1))
    if line:
        @pl.when(inner)
        def _():
            signal(far, z_peer(3))
            pl.semaphore_wait(far, 1)
            signal(far, z_peer(1))
    for copy in loads[4:]:
        copy.wait()

    def swap_tiles():
        push(a_full.at[pl.ds(0, tr), pl.ds(0, half)],
             a_full.at[pl.ds(tr, tr), pl.ds(half, half)], sent_s.at[2], ex_r.at[1], mate)
        push(a_full.at[pl.ds(0, tr), pl.ds(half, half)],
             a_full.at[pl.ds(tr, tr), pl.ds(0, half)], sent_s.at[3], ex_r.at[2], mate)
        push(grads.at[pl.ds(0, tr)], grads.at[pl.ds(tr, tr)], sent_s.at[4], ex_r.at[3], mate)

    if EARLY:
        swap_tiles()

    def hs(k):
        return slice(k * hc, (k + 1) * hc)

    def send_terms(k, make, out, into, ss, rr):
        for r in order:
            out[k, r - 1] = make(k, r).astype(BF16)
            push(out.at[k, r - 1], into.at[k, r - 1], ss, rr.at[k, r - 1], z_peer(r))
        return make(k, 0)

    def take_terms(k, kept, into, rr):
        for r in order:
            landed(into.at[k, r - 1], rr.at[k, r - 1])
        for r in order:
            kept = kept + into[k, r - 1].astype(F32)
        return kept.astype(BF16)

    def gather_send(k, buf, ss, rr):
        for r in order:
            push(buf.at[k, 0], buf.at[k, r], ss, rr.at[k, r - 1], z_peer(r))

    def forward(k, r, buf, ss, rr):
        push(buf.at[k, r], buf.at[k, zs + r], ss, rr.at[k, r], mate)

    def gather_pass(k, buf, rr, ss, ff):
        for r in order:
            landed(buf.at[k, r], rr.at[k, r - 1])
            forward(k, r, buf, ss, ff)

    def project(k, r):
        if k == 0:
            landed(x_pair.at[r, pl.ds(fd, fd)], x_r.at[r])
        return tn(x_pair[r], w_pair[:, hs(k)])

    landed(w_pair.at[pl.ds(fd, fd)], ex_r.at[0])
    if line:
        @pl.when(outer)
        def _():
            pl.semaphore_wait(far, 1)
    kept = [send_terms(k, project, rs_out, rs_in, sent_s.at[5], rs_r) for k in ks]
    if not EARLY:
        mask_tiles()
        swap_tiles()
    landed(a_full.at[pl.ds(tr, tr), pl.ds(half, half)], ex_r.at[1])
    landed(a_full.at[pl.ds(tr, tr), pl.ds(0, half)], ex_r.at[2])
    row_scale = lax.rsqrt(jnp.sum(a_full[...].astype(F32), axis=1, keepdims=True))
    landed(grads.at[pl.ds(tr, tr)], ex_r.at[3])
    for k in ks:
        gath[k, 0] = take_terms(k, kept[k], rs_in, rs_r)
        gather_send(k, gath, sent_s.at[6], ag_r)
        forward(k, 0, gath, sent_s.at[7], fa_r)

    def terms(k, r):
        return tn(a_full[:, r * tr:(r + 1) * tr], sc_full[k])

    kept = []
    for k in ks:
        gather_pass(k, gath, ag_r, sent_s.at[7], fa_r)
        summed = nn(a_full[:, 0:half], gath[k, 0:zs].reshape(half, hc))
        for r in [0] + order:
            landed(gath.at[k, zs + r], fa_r.at[k, r])
        summed = summed + nn(a_full[:, half:], gath[k, zs:].reshape(half, hc))
        v = summed * row_scale + bias[:, hs(k)]
        v2 = v * v
        t = jnp.tanh(ROOT * (v + 0.044715 * v2 * v))
        slope = 0.5 * (1.0 + t) + 0.5 * v * (1.0 - t * t) * (ROOT * (1.0 + 3 * 0.044715 * v2))
        grad_pre = grads[:, hs(k)].astype(F32) * slope
        sc_full[k] = (grad_pre * row_scale).astype(BF16)
        kept.append(send_terms(k, terms, rt_out, rt_in, sent_s.at[8], rt_r))
        hidden[:, hs(k)] = (0.5 * v[0:tr] * (1.0 + t[0:tr])).astype(BF16)

    for k in ks:
        ggath[k, 0] = take_terms(k, kept[k], rt_in, rt_r)
        gather_send(k, ggath, sent_s.at[9], gg_r)
        forward(k, 0, ggath, sent_s.at[10], fw_r)
    scale = 1.0 / math.sqrt(total)

    if square:
        pl.semaphore_wait(aside, 1)
    for k in ks:
        gather_pass(k, ggath, gg_r, sent_s.at[10], fw_r)
        acc = jnp.zeros((fd, hc), F32)
        for r in range(zs):
            acc = acc + nn(x_pair[r, 0:fd, :], ggath[k, r])
        for r in [0] + order:
            landed(ggath.at[k, zs + r], fw_r.at[k, r])
            acc = acc + nn(x_send[r], ggath[k, zs + r])
        wg_in[k, 0] = acc.astype(BF16)
        for n in reversed(range(1, nodes)):
            push(wg_in.at[k, 0], wg_in.at[k, n], sent_s.at[11], wg_r.at[k, n - 1], n_peer(n))
    for r in range(zs):
        for parity, at in ((core, r), (1 - core, zs + r)):
            total_rows = nt(weight[:, hs(0)], ggath[0, at])
            for k in range(1, CHUNKS):
                total_rows = total_rows + nt(weight[:, hs(k)], ggath[k, at])
            grad_feat[:, pl.ds(rows_of(r, parity), tr)] = total_rows.astype(BF16)
    for i, ref in enumerate((
            weight, x_send, a_full.at[pl.ds(0, tr), pl.ds(0, half)],
            a_full.at[pl.ds(0, tr), pl.ds(half, half)], grads.at[pl.ds(0, tr)],
            rs_out, rs_out, gath.at[:, pl.ds(0, zs)], rt_out, rt_out,
            ggath.at[:, pl.ds(0, zs)])):
        landed(ref, sent_s.at[i])
    for k in ks:
        for n in range(1, nodes):
            landed(wg_in.at[k, n], wg_r.at[k, n - 1])
        level = [wg_in[k, n].astype(F32) for n in range(nodes)]
        while len(level) > 1:
            level = [level[i] + level[i + 1] for i in range(0, len(level), 2)]
        weight_grad[:, hs(k)] = level[0] * scale
    landed(wg_in.at[:, pl.ds(1, nodes - 1)], sent_s.at[11])


def write_out(a, b, c, a_out, b_out, c_out, sems):
    pairs = ((a, a_out), (b, b_out), (c, c_out))
    copies = [pltpu.make_async_copy(x, y, sems.at[i]) for i, (x, y) in enumerate(pairs)]
    for copy in copies:
        copy.start()
    for copy in copies:
        copy.wait()


def body(node_features, weight, out_bias, edge_tiles, tile_column, tile_count, grad_hidden):
    fd, _, rows = node_features.shape
    blocks = lax.axis_size("feat")
    nodes = lax.axis_size("node")
    zs = blocks // 2
    tr = rows // blocks
    hw = weight.shape[1]
    hc = hw // CHUNKS
    slots = edge_tiles.shape[2]
    sizes = (zs, nodes, slots, tr, fd, hw, nodes * rows)
    vmem = pl.BlockSpec(memory_space=pltpu.VMEM)
    hbm = pl.BlockSpec(memory_space=pltpu.HBM)
    dma = pltpu.SemaphoreType.DMA
    c = CHUNKS
    scratch = [
        pltpu.SMEM((1, 1, slots), jnp.int32),
        pltpu.SMEM((1, 1), jnp.int32),
        pltpu.VMEM((fd, hw), BF16),
        pltpu.VMEM((1, hw), F32),
        pltpu.VMEM((slots, tr, tr), BF16),
        pltpu.VMEM((2 * tr, hw), BF16),
        pltpu.VMEM((zs, fd, tr), BF16),
        pltpu.VMEM((zs, 2 * fd, tr), BF16),
        pltpu.VMEM((2 * fd, hw), BF16),
        pltpu.VMEM((2 * tr, 2 * zs * tr), BF16),
        pltpu.VMEM((c, zs - 1, tr, hc), BF16),
        pltpu.VMEM((c, zs - 1, tr, hc), BF16),
        pltpu.VMEM((c, 2 * zs, tr, hc), BF16),
        pltpu.VMEM((c, 2 * tr, hc), BF16),
        pltpu.VMEM((c, zs - 1, tr, hc), BF16),
        pltpu.VMEM((c, zs - 1, tr, hc), BF16),
        pltpu.VMEM((c, 2 * zs, tr, hc), BF16),
        pltpu.VMEM((c, nodes, fd, hc), BF16),
        dma((6,)),
        dma,
        dma,
        dma((12,)),
        dma((4,)),
        dma((zs,)),
        dma((c, zs - 1)),
        dma((c, zs - 1)),
        dma((c, zs)),
        dma((c, zs - 1)),
        dma((c, zs - 1)),
        dma((c, zs)),
        dma((c, nodes - 1)),
        pltpu.SemaphoreType.REGULAR,
        pltpu.SemaphoreType.REGULAR,
    ]
    hidden, grad_feat, weight_grad = pl.pallas_call(
        functools.partial(kernel, sizes),
        out_shape=(
            jax.ShapeDtypeStruct((tr, hw), BF16),
            jax.ShapeDtypeStruct((fd, rows), BF16),
            jax.ShapeDtypeStruct((fd, hw), F32),
        ),
        in_specs=[hbm] * 7,
        out_specs=(vmem, vmem, vmem),
        scratch_shapes=scratch,
        compiler_params=pltpu.CompilerParams(
            collective_id=0, has_side_effects=True, vmem_limit_bytes=63 * 1024 * 1024
        ),
        name="sage",
    )(
        tile_column,
        tile_count,
        node_features.reshape(fd, rows),
        weight,
        out_bias.reshape(1, hw),
        edge_tiles.reshape(slots, tr, tr),
        grad_hidden.reshape(tr, hw),
    )
    hidden, grad_feat, weight_grad = pl.pallas_call(
        write_out,
        out_shape=(
            jax.ShapeDtypeStruct((tr, hw), BF16),
            jax.ShapeDtypeStruct((fd, rows), BF16),
            jax.ShapeDtypeStruct((fd, hw), F32),
        ),
        in_specs=[vmem] * 3,
        out_specs=(hbm,) * 3,
        scratch_shapes=[dma((3,))],
        name="write_out",
    )(hidden, grad_feat, weight_grad)
    return (hidden[None], grad_feat[:, None, :], weight_grad)


def solution(mesh):
    return jax.shard_map(
        body,
        mesh=mesh,
        in_specs=(
            P("feat", "node", None),
            P("feat", None),
            P(),
            P("node", "feat", None, None, None),
            P("node", "feat", None),
            P("node", "feat"),
            P("node", "feat", None),
        ),
        out_specs=(P("node", "feat", None), P("feat", "node", None), P("feat", None)),
        check_vma=False,
    )
```

```python
import functools
import math

import jax
import jax.numpy as jnp
from jax import lax
from jax.experimental import pallas as pl
from jax.experimental.pallas import tpu as pltpu
from jax.sharding import PartitionSpec as P

MESH = pl.DeviceIdType.MESH
F32 = jnp.float32
BF16 = jnp.bfloat16
CHUNKS = 2
EARLY = False
ROOT = math.sqrt(2.0 / math.pi)


def flip(index, bit):
    return index + bit * (1 - 2 * ((index // bit) % 2))


def flip_many(index, mask, steps):
    for j in range(steps):
        if (mask >> j) & 1:
            index = flip(index, 1 << j)
    return index


def tn(a, b):
    return lax.dot_general(a, b, (((0,), (0,)), ((), ())), preferred_element_type=F32)


def nt(a, b):
    return lax.dot_general(a, b, (((1,), (1,)), ((), ())), preferred_element_type=F32)


def nn(a, b):
    return lax.dot_general(a, b, (((1,), (0,)), ((), ())), preferred_element_type=F32)


def landed(ref, sem):
    pltpu.make_async_copy(ref, ref, sem).wait()


def kernel(sizes, cols_hbm, count_hbm, feats, weight_hbm, bias_hbm, tiles_hbm, grad_hbm,
           hidden, grad_feat, weight_grad,
           cols, count, weight, bias, tiles, grads,
           x_send, x_pair, w_pair, a_full, rs_out, rs_in, gath, sc_full, rt_out, rt_in,
           ggath, wg_in,
           small_s, xa_s, xb_s, sent_s, ex_r, x_r, rs_r, ag_r, fa_r, rt_r, gg_r, fw_r, wg_r,
           far, aside):
    zs, nodes, slots, tr, fd, hw, total = sizes
    zbits, nbits = zs.bit_length() - 1, nodes.bit_length() - 1
    hc = hw // CHUNKS
    ks = range(CHUNKS)
    feat_at = lax.axis_index("feat")
    node_at = lax.axis_index("node")
    core = feat_at % 2
    z = feat_at // 2
    mate = {"feat": z * 2 + 1 - core}
    line = zs == 4
    square = nodes == 4
    inner = jnp.logical_or(z == 1, z == 2)
    outer = jnp.logical_not(inner)

    zrel = [flip_many(z, r, zbits) for r in range(zs)]

    def z_peer(r):
        return {"feat": zrel[r] * 2 + core}

    def n_peer(n):
        return {"node": flip_many(node_at, n, nbits)}

    def push(src, dst, ss, rr, dev):
        pltpu.make_async_remote_copy(
            src_ref=src, dst_ref=dst, send_sem=ss, recv_sem=rr,
            device_id=dev, device_id_type=MESH).start()

    def signal(sem, dev):
        pl.semaphore_signal(sem, inc=1, device_id=dev, device_id_type=MESH)

    barrier = pltpu.get_barrier_semaphore()
    near_n = [1, 2] if square else list(range(1, nodes))
    near_z = [1] if line else list(range(1, zs))
    for r in near_z:
        signal(barrier, z_peer(r))
    if line:
        @pl.when(inner)
        def _():
            signal(barrier, z_peer(3))
    for n in near_n:
        signal(barrier, n_peer(n))
    signal(barrier, mate)

    def rows_of(r, parity):
        return pl.multiple_of((zrel[r] * 2 + parity) * tr, tr)

    def fetch(src, dst, sem):
        copy = pltpu.make_async_copy(src, dst, sem)
        copy.start()
        return copy

    order = list(reversed(range(1, zs)))
    loads = [fetch(src, dst, small_s.at[i]) for i, (src, dst) in enumerate((
        (weight_hbm, weight), (cols_hbm, cols), (count_hbm, count), (tiles_hbm, tiles),
        (bias_hbm, bias), (grad_hbm, grads.at[pl.ds(0, tr)])))]
    for r in range(zs):
        fetch(feats.at[:, pl.ds(rows_of(r, core), tr)], x_pair.at[r, pl.ds(0, fd)], xa_s)
    for r in range(zs):
        fetch(feats.at[:, pl.ds(rows_of(r, 1 - core), tr)], x_send.at[r], xb_s)
    loads[0].wait()
    w_pair[0:fd, :] = weight[...]
    for i in range(1, 4):
        loads[i].wait()
    live = count[0, 0]

    def listed(block):
        where = jnp.int32(0)
        alive = jnp.int32(0)
        for s in range(slots):
            hit = cols[0, 0, s] == block
            where = jnp.where(hit, s, where)
            alive = jnp.where(hit, jnp.where(s < live, 1, 0), alive)
        return tiles[where] * alive.astype(BF16)

    half = zs * tr

    def mask_tiles():
        for p in range(2):
            for r in range(zs):
                parity = core if p == 0 else 1 - core
                at = p * half + r * tr
                a_full[0:tr, at:at + tr] = listed(zrel[r] * 2 + parity)

    if EARLY:
        mask_tiles()
    landed(x_pair.at[:, pl.ds(0, fd)], xa_s)
    landed(x_send, xb_s)

    greeted = 1 + len(near_n) + len(near_z)
    if line:
        greeted = greeted + jnp.where(inner, 1, 0)
    pl.semaphore_wait(barrier, greeted)
    push(weight, w_pair.at[pl.ds(fd, fd)], sent_s.at[0], ex_r.at[0], mate)
    for r in order + [0]:
        push(x_send.at[r], x_pair.at[r, pl.ds(fd, fd)], sent_s.at[1], x_r.at[r], mate)
    if square:
        signal(aside, n_peer(1))
    if line:
        @pl.when(inner)
        def _():
            signal(far, z_peer(3))
            pl.semaphore_wait(far, 1)
            signal(far, z_peer(1))
    for copy in loads[4:]:
        copy.wait()

    def swap_tiles():
        push(a_full.at[pl.ds(0, tr), pl.ds(0, half)],
             a_full.at[pl.ds(tr, tr), pl.ds(half, half)], sent_s.at[2], ex_r.at[1], mate)
        push(a_full.at[pl.ds(0, tr), pl.ds(half, half)],
             a_full.at[pl.ds(tr, tr), pl.ds(0, half)], sent_s.at[3], ex_r.at[2], mate)
        push(grads.at[pl.ds(0, tr)], grads.at[pl.ds(tr, tr)], sent_s.at[4], ex_r.at[3], mate)

    if EARLY:
        swap_tiles()

    def hs(k):
        return slice(k * hc, (k + 1) * hc)

    def send_terms(k, make, out, into, ss, rr):
        for r in order:
            out[k, r - 1] = make(k, r).astype(BF16)
            push(out.at[k, r - 1], into.at[k, r - 1], ss, rr.at[k, r - 1], z_peer(r))
        return make(k, 0)

    def take_terms(k, kept, into, rr):
        for r in order:
            landed(into.at[k, r - 1], rr.at[k, r - 1])
        for r in order:
            kept = kept + into[k, r - 1].astype(F32)
        return kept.astype(BF16)

    def gather_send(k, buf, ss, rr):
        for r in order:
            push(buf.at[k, 0], buf.at[k, r], ss, rr.at[k, r - 1], z_peer(r))

    def forward(k, r, buf, ss, rr):
        push(buf.at[k, r], buf.at[k, zs + r], ss, rr.at[k, r], mate)

    def gather_pass(k, buf, rr, ss, ff):
        for r in order:
            landed(buf.at[k, r], rr.at[k, r - 1])
            forward(k, r, buf, ss, ff)

    def project(k, r):
        if k == 0:
            landed(x_pair.at[r, pl.ds(fd, fd)], x_r.at[r])
        return tn(x_pair[r], w_pair[:, hs(k)])

    landed(w_pair.at[pl.ds(fd, fd)], ex_r.at[0])
    if line:
        @pl.when(outer)
        def _():
            pl.semaphore_wait(far, 1)
    kept = [send_terms(k, project, rs_out, rs_in, sent_s.at[5], rs_r) for k in ks]
    if not EARLY:
        mask_tiles()
        swap_tiles()
    landed(a_full.at[pl.ds(tr, tr), pl.ds(half, half)], ex_r.at[1])
    landed(a_full.at[pl.ds(tr, tr), pl.ds(0, half)], ex_r.at[2])
    row_scale = lax.rsqrt(jnp.sum(a_full[...].astype(F32), axis=1, keepdims=True))
    landed(grads.at[pl.ds(tr, tr)], ex_r.at[3])
    for k in ks:
        gath[k, 0] = take_terms(k, kept[k], rs_in, rs_r)
        gather_send(k, gath, sent_s.at[6], ag_r)
        forward(k, 0, gath, sent_s.at[7], fa_r)

    def terms(k, r):
        return tn(a_full[:, r * tr:(r + 1) * tr], sc_full[k])

    kept = []
    for k in ks:
        gather_pass(k, gath, ag_r, sent_s.at[7], fa_r)
        summed = nn(a_full[:, 0:half], gath[k, 0:zs].reshape(half, hc))
        for r in [0] + order:
            landed(gath.at[k, zs + r], fa_r.at[k, r])
        summed = summed + nn(a_full[:, half:], gath[k, zs:].reshape(half, hc))
        v = summed * row_scale + bias[:, hs(k)]
        v2 = v * v
        t = jnp.tanh(ROOT * (v + 0.044715 * v2 * v))
        slope = 0.5 * (1.0 + t) + 0.5 * v * (1.0 - t * t) * (ROOT * (1.0 + 3 * 0.044715 * v2))
        grad_pre = grads[:, hs(k)].astype(F32) * slope
        sc_full[k] = (grad_pre * row_scale).astype(BF16)
        kept.append(send_terms(k, terms, rt_out, rt_in, sent_s.at[8], rt_r))
        hidden[:, hs(k)] = (0.5 * v[0:tr] * (1.0 + t[0:tr])).astype(BF16)

    for k in ks:
        ggath[k, 0] = take_terms(k, kept[k], rt_in, rt_r)
        gather_send(k, ggath, sent_s.at[9], gg_r)
        forward(k, 0, ggath, sent_s.at[10], fw_r)
    scale = 1.0 / math.sqrt(total)

    if square:
        pl.semaphore_wait(aside, 1)
    for k in ks:
        gather_pass(k, ggath, gg_r, sent_s.at[10], fw_r)
        acc = jnp.zeros((fd, hc), F32)
        for r in range(zs):
            acc = acc + nn(x_pair[r, 0:fd, :], ggath[k, r])
        for r in [0] + order:
            landed(ggath.at[k, zs + r], fw_r.at[k, r])
            acc = acc + nn(x_send[r], ggath[k, zs + r])
        wg_in[k, 0] = acc.astype(BF16)
        for n in reversed(range(1, nodes)):
            push(wg_in.at[k, 0], wg_in.at[k, n], sent_s.at[11], wg_r.at[k, n - 1], n_peer(n))
    for r in range(zs):
        for parity, at in ((core, r), (1 - core, zs + r)):
            total_rows = nt(weight[:, hs(0)], ggath[0, at])
            for k in range(1, CHUNKS):
                total_rows = total_rows + nt(weight[:, hs(k)], ggath[k, at])
            grad_feat[:, pl.ds(rows_of(r, parity), tr)] = total_rows.astype(BF16)
    for i, ref in enumerate((
            weight, x_send, a_full.at[pl.ds(0, tr), pl.ds(0, half)],
            a_full.at[pl.ds(0, tr), pl.ds(half, half)], grads.at[pl.ds(0, tr)],
            rs_out, rs_out, gath.at[:, pl.ds(0, zs)], rt_out, rt_out,
            ggath.at[:, pl.ds(0, zs)])):
        landed(ref, sent_s.at[i])
    for k in ks:
        for n in range(1, nodes):
            landed(wg_in.at[k, n], wg_r.at[k, n - 1])
        level = [wg_in[k, n].astype(F32) for n in range(nodes)]
        while len(level) > 1:
            level = [level[i] + level[i + 1] for i in range(0, len(level), 2)]
        weight_grad[:, hs(k)] = level[0] * scale
    landed(wg_in.at[:, pl.ds(1, nodes - 1)], sent_s.at[11])


def write_out(a, b, c, a_out, b_out, c_out, sems):
    pairs = ((a, a_out), (b, b_out), (c, c_out))
    copies = [pltpu.make_async_copy(x, y, sems.at[i]) for i, (x, y) in enumerate(pairs)]
    for copy in copies:
        copy.start()
    for copy in copies:
        copy.wait()


def body(node_features, weight, out_bias, edge_tiles, tile_column, tile_count, grad_hidden):
    fd, _, rows = node_features.shape
    blocks = lax.axis_size("feat")
    nodes = lax.axis_size("node")
    zs = blocks // 2
    tr = rows // blocks
    hw = weight.shape[1]
    hc = hw // CHUNKS
    slots = edge_tiles.shape[2]
    sizes = (zs, nodes, slots, tr, fd, hw, nodes * rows)
    vmem = pl.BlockSpec(memory_space=pltpu.VMEM)
    hbm = pl.BlockSpec(memory_space=pltpu.HBM)
    dma = pltpu.SemaphoreType.DMA
    c = CHUNKS
    scratch = [
        pltpu.SMEM((1, 1, slots), jnp.int32),
        pltpu.SMEM((1, 1), jnp.int32),
        pltpu.VMEM((fd, hw), BF16),
        pltpu.VMEM((1, hw), F32),
        pltpu.VMEM((slots, tr, tr), BF16),
        pltpu.VMEM((2 * tr, hw), BF16),
        pltpu.VMEM((zs, fd, tr), BF16),
        pltpu.VMEM((zs, 2 * fd, tr), BF16),
        pltpu.VMEM((2 * fd, hw), BF16),
        pltpu.VMEM((2 * tr, 2 * zs * tr), BF16),
        pltpu.VMEM((c, zs - 1, tr, hc), BF16),
        pltpu.VMEM((c, zs - 1, tr, hc), BF16),
        pltpu.VMEM((c, 2 * zs, tr, hc), BF16),
        pltpu.VMEM((c, 2 * tr, hc), BF16),
        pltpu.VMEM((c, zs - 1, tr, hc), BF16),
        pltpu.VMEM((c, zs - 1, tr, hc), BF16),
        pltpu.VMEM((c, 2 * zs, tr, hc), BF16),
        pltpu.VMEM((c, nodes, fd, hc), BF16),
        dma((6,)),
        dma,
        dma,
        dma((12,)),
        dma((4,)),
        dma((zs,)),
        dma((c, zs - 1)),
        dma((c, zs - 1)),
        dma((c, zs)),
        dma((c, zs - 1)),
        dma((c, zs - 1)),
        dma((c, zs)),
        dma((c, nodes - 1)),
        pltpu.SemaphoreType.REGULAR,
        pltpu.SemaphoreType.REGULAR,
    ]
    hidden, grad_feat, weight_grad = pl.pallas_call(
        functools.partial(kernel, sizes),
        out_shape=(
            pltpu.VMEM((tr, hw), BF16),
            pltpu.VMEM((fd, rows), BF16),
            pltpu.VMEM((fd, hw), F32),
        ),
        in_specs=[hbm] * 7,
        out_specs=(vmem, vmem, vmem),
        scratch_shapes=scratch,
        compiler_params=pltpu.CompilerParams(
            collective_id=0, has_side_effects=True, vmem_limit_bytes=62 * 1024 * 1024
        ),
        name="sage",
    )(
        tile_column,
        tile_count,
        node_features.reshape(fd, rows),
        weight,
        out_bias.reshape(1, hw),
        edge_tiles.reshape(slots, tr, tr),
        grad_hidden.reshape(tr, hw),
    )
    hidden, grad_feat, weight_grad = pl.pallas_call(
        write_out,
        out_shape=(
            jax.ShapeDtypeStruct((tr, hw), BF16),
            jax.ShapeDtypeStruct((fd, rows), BF16),
            jax.ShapeDtypeStruct((fd, hw), F32),
        ),
        in_specs=[vmem] * 3,
        out_specs=(hbm,) * 3,
        scratch_shapes=[dma((3,))],
        name="write_out",
    )(*(pltpu.with_memory_space_constraint(x, pltpu.VMEM)
        for x in (hidden, grad_feat, weight_grad)))
    return (hidden[None], grad_feat[:, None, :], weight_grad)


def solution(mesh):
    return jax.shard_map(
        body,
        mesh=mesh,
        in_specs=(
            P("feat", "node", None),
            P("feat", None),
            P(),
            P("node", "feat", None, None, None),
            P("node", "feat", None),
            P("node", "feat"),
            P("node", "feat", None),
        ),
        out_specs=(P("node", "feat", None), P("feat", "node", None), P("feat", None)),
        check_vma=False,
    )
```

```python
import functools
import math

import jax
import jax.numpy as jnp
from jax import lax
from jax.experimental import pallas as pl
from jax.experimental.pallas import tpu as pltpu
from jax.sharding import PartitionSpec as P

MESH = pl.DeviceIdType.MESH
F32 = jnp.float32
BF16 = jnp.bfloat16
CHUNKS = 2
ROOT = math.sqrt(2.0 / math.pi)


def flip(index, bit):
    return index + bit * (1 - 2 * ((index // bit) % 2))


def flip_many(index, mask, steps):
    for j in range(steps):
        if (mask >> j) & 1:
            index = flip(index, 1 << j)
    return index


def tn(a, b):
    return lax.dot_general(a, b, (((0,), (0,)), ((), ())), preferred_element_type=F32)


def nt(a, b):
    return lax.dot_general(a, b, (((1,), (1,)), ((), ())), preferred_element_type=F32)


def nn(a, b):
    return lax.dot_general(a, b, (((1,), (0,)), ((), ())), preferred_element_type=F32)


def landed(ref, sem):
    pltpu.make_async_copy(ref, ref, sem).wait()


def kernel(sizes, cols_hbm, count_hbm, feats, weight_hbm, bias_hbm, tiles_hbm, grad_hbm,
           hidden, grad_feat, weight_grad,
           cols, count, weight, bias, tiles, grads,
           x_send, x_pair, w_pair, a_full, rs_out, rs_in, gath, sc_full, rt_out, rt_in,
           ggath, wg_in,
           small_s, xa_s, xb_s, sent_s, ex_r, x_r, rs_r, ag_r, fa_r, rt_r, gg_r, fw_r, wg_r,
           far, aside):
    zs, nodes, slots, tr, fd, hw, total = sizes
    zbits, nbits = zs.bit_length() - 1, nodes.bit_length() - 1
    hc = hw // CHUNKS
    ks = range(CHUNKS)
    feat_at = lax.axis_index("feat")
    node_at = lax.axis_index("node")
    core = feat_at % 2
    z = feat_at // 2
    mate = {"feat": z * 2 + 1 - core}
    line = zs == 4
    square = nodes == 4
    inner = jnp.logical_or(z == 1, z == 2)
    outer = jnp.logical_not(inner)

    zrel = [flip_many(z, r, zbits) for r in range(zs)]

    def z_peer(r):
        return {"feat": zrel[r] * 2 + core}

    def n_peer(n):
        return {"node": flip_many(node_at, n, nbits)}

    def push(src, dst, ss, rr, dev):
        pltpu.make_async_remote_copy(
            src_ref=src, dst_ref=dst, send_sem=ss, recv_sem=rr,
            device_id=dev, device_id_type=MESH).start()

    def signal(sem, dev):
        pl.semaphore_signal(sem, inc=1, device_id=dev, device_id_type=MESH)

    barrier = pltpu.get_barrier_semaphore()
    near_n = [1, 2] if square else list(range(1, nodes))
    near_z = [1] if line else list(range(1, zs))
    for r in near_z:
        signal(barrier, z_peer(r))
    if line:
        @pl.when(inner)
        def _():
            signal(barrier, z_peer(3))
    for n in near_n:
        signal(barrier, n_peer(n))
    signal(barrier, mate)

    def rows_of(r, parity):
        return pl.multiple_of((zrel[r] * 2 + parity) * tr, tr)

    def fetch(src, dst, sem):
        copy = pltpu.make_async_copy(src, dst, sem)
        copy.start()
        return copy

    order = list(reversed(range(1, zs)))
    loads = [fetch(src, dst, small_s.at[i]) for i, (src, dst) in enumerate((
        (weight_hbm, weight), (cols_hbm, cols), (count_hbm, count), (tiles_hbm, tiles),
        (bias_hbm, bias), (grad_hbm, grads.at[pl.ds(0, tr)])))]
    for r in range(zs):
        fetch(feats.at[:, pl.ds(rows_of(r, core), tr)], x_pair.at[r, pl.ds(0, fd)], xa_s)
    for r in range(zs):
        fetch(feats.at[:, pl.ds(rows_of(r, 1 - core), tr)], x_send.at[r], xb_s)
    loads[0].wait()
    w_pair[0:fd, :] = weight[...]
    for i in range(1, 4):
        loads[i].wait()
    live = count[0, 0]

    def listed(block):
        where = jnp.int32(0)
        alive = jnp.int32(0)
        for s in range(slots):
            hit = cols[0, 0, s] == block
            where = jnp.where(hit, s, where)
            alive = jnp.where(hit, jnp.where(s < live, 1, 0), alive)
        return tiles[where] * alive.astype(BF16)

    half = zs * tr

    def mask_tiles():
        for p in range(2):
            for r in range(zs):
                parity = core if p == 0 else 1 - core
                at = p * half + r * tr
                a_full[0:tr, at:at + tr] = listed(zrel[r] * 2 + parity)

    landed(x_pair.at[:, pl.ds(0, fd)], xa_s)
    landed(x_send, xb_s)

    greeted = 1 + len(near_n) + len(near_z)
    if line:
        greeted = greeted + jnp.where(inner, 1, 0)
    pl.semaphore_wait(barrier, greeted)
    push(weight, w_pair.at[pl.ds(fd, fd)], sent_s.at[0], ex_r.at[0], mate)
    for r in order + [0]:
        push(x_send.at[r], x_pair.at[r, pl.ds(fd, fd)], sent_s.at[1], x_r.at[r], mate)
    if square:
        signal(aside, n_peer(1))
    if line:
        @pl.when(inner)
        def _():
            signal(far, z_peer(3))
            pl.semaphore_wait(far, 1)
            signal(far, z_peer(1))
    for copy in loads[4:]:
        copy.wait()

    def swap_tiles():
        push(a_full.at[pl.ds(0, tr), pl.ds(0, half)],
             a_full.at[pl.ds(tr, tr), pl.ds(half, half)], sent_s.at[2], ex_r.at[1], mate)
        push(a_full.at[pl.ds(0, tr), pl.ds(half, half)],
             a_full.at[pl.ds(tr, tr), pl.ds(0, half)], sent_s.at[3], ex_r.at[2], mate)
        push(grads.at[pl.ds(0, tr)], grads.at[pl.ds(tr, tr)], sent_s.at[4], ex_r.at[3], mate)

    def hs(k):
        return slice(k * hc, (k + 1) * hc)

    def send_terms(k, make, out, into, ss, rr):
        for r in order:
            out[k, r - 1] = make(k, r).astype(BF16)
            push(out.at[k, r - 1], into.at[k, r - 1], ss, rr.at[k], z_peer(r))
        return make(k, 0)

    def take_terms(k, kept, into, rr):
        landed(into.at[k], rr.at[k])
        for r in order:
            kept = kept + into[k, r - 1].astype(F32)
        return kept.astype(BF16)

    def gather_send(k, buf, ss, rr):
        for r in order:
            push(buf.at[k, 0], buf.at[k, r], ss, rr.at[k, r - 1], z_peer(r))

    def forward(k, r, buf, ss, rr):
        push(buf.at[k, r], buf.at[k, zs + r], ss, rr.at[k], mate)

    def gather_pass(k, buf, rr, ss, ff):
        for r in order:
            landed(buf.at[k, r], rr.at[k, r - 1])
        push(buf.at[k, pl.ds(1, zs - 1)], buf.at[k, pl.ds(zs + 1, zs - 1)], ss, ff.at[k], mate)

    def project(k, r):
        if k == 0:
            landed(x_pair.at[r, pl.ds(fd, fd)], x_r.at[r])
        return tn(x_pair[r], w_pair[:, hs(k)])

    landed(w_pair.at[pl.ds(fd, fd)], ex_r.at[0])
    if line:
        @pl.when(outer)
        def _():
            pl.semaphore_wait(far, 1)
    kept = [send_terms(k, project, rs_out, rs_in, sent_s.at[5], rs_r) for k in ks]
    mask_tiles()
    swap_tiles()
    landed(a_full.at[pl.ds(tr, tr), pl.ds(half, half)], ex_r.at[1])
    landed(a_full.at[pl.ds(tr, tr), pl.ds(0, half)], ex_r.at[2])
    row_scale = lax.rsqrt(jnp.sum(a_full[...].astype(F32), axis=1, keepdims=True))
    landed(grads.at[pl.ds(tr, tr)], ex_r.at[3])
    for k in ks:
        gath[k, 0] = take_terms(k, kept[k], rs_in, rs_r)
        gather_send(k, gath, sent_s.at[6], ag_r)
        forward(k, 0, gath, sent_s.at[7], fa_r)

    def terms(k, r):
        return tn(a_full[:, r * tr:(r + 1) * tr], sc_full[k])

    kept = []
    for k in ks:
        gather_pass(k, gath, ag_r, sent_s.at[7], fa_r)
        summed = nn(a_full[:, 0:half], gath[k, 0:zs].reshape(half, hc))
        landed(gath.at[k, pl.ds(zs, zs)], fa_r.at[k])
        summed = summed + nn(a_full[:, half:], gath[k, zs:].reshape(half, hc))
        v = summed * row_scale + bias[:, hs(k)]
        v2 = v * v
        t = jnp.tanh(ROOT * (v + 0.044715 * v2 * v))
        slope = 0.5 * (1.0 + t) + 0.5 * v * (1.0 - t * t) * (ROOT * (1.0 + 3 * 0.044715 * v2))
        grad_pre = grads[:, hs(k)].astype(F32) * slope
        sc_full[k] = (grad_pre * row_scale).astype(BF16)
        kept.append(send_terms(k, terms, rt_out, rt_in, sent_s.at[8], rt_r))
        hidden[:, hs(k)] = (0.5 * v[0:tr] * (1.0 + t[0:tr])).astype(BF16)

    for k in ks:
        ggath[k, 0] = take_terms(k, kept[k], rt_in, rt_r)
        gather_send(k, ggath, sent_s.at[9], gg_r)
        forward(k, 0, ggath, sent_s.at[10], fw_r)
    scale = 1.0 / math.sqrt(total)

    if square:
        pl.semaphore_wait(aside, 1)
    for k in ks:
        gather_pass(k, ggath, gg_r, sent_s.at[10], fw_r)
        acc = jnp.zeros((fd, hc), F32)
        for r in range(zs):
            acc = acc + nn(x_pair[r, 0:fd, :], ggath[k, r])
        landed(ggath.at[k, pl.ds(zs, zs)], fw_r.at[k])
        for r in range(zs):
            acc = acc + nn(x_send[r], ggath[k, zs + r])
        wg_in[k, 0] = acc.astype(BF16)
        for n in reversed(range(1, nodes)):
            push(wg_in.at[k, 0], wg_in.at[k, n], sent_s.at[11], wg_r.at[k], n_peer(n))
    for r in range(zs):
        for parity, at in ((core, r), (1 - core, zs + r)):
            total_rows = nt(weight[:, hs(0)], ggath[0, at])
            for k in range(1, CHUNKS):
                total_rows = total_rows + nt(weight[:, hs(k)], ggath[k, at])
            grad_feat[:, pl.ds(rows_of(r, parity), tr)] = total_rows.astype(BF16)
    for i, ref in enumerate((
            weight, x_send, a_full.at[pl.ds(0, tr), pl.ds(0, half)],
            a_full.at[pl.ds(0, tr), pl.ds(half, half)], grads.at[pl.ds(0, tr)],
            rs_out, rs_out, gath.at[:, pl.ds(0, zs)], rt_out, rt_out,
            ggath.at[:, pl.ds(0, zs)])):
        landed(ref, sent_s.at[i])
    for k in ks:
        landed(wg_in.at[k, pl.ds(1, nodes - 1)], wg_r.at[k])
        level = [wg_in[k, n].astype(F32) for n in range(nodes)]
        while len(level) > 1:
            level = [level[i] + level[i + 1] for i in range(0, len(level), 2)]
        weight_grad[:, hs(k)] = level[0] * scale
    landed(wg_in.at[:, pl.ds(1, nodes - 1)], sent_s.at[11])


def write_out(a, b, c, a_out, b_out, c_out, sems):
    pairs = ((a, a_out), (b, b_out), (c, c_out))
    copies = [pltpu.make_async_copy(x, y, sems.at[i]) for i, (x, y) in enumerate(pairs)]
    for copy in copies:
        copy.start()
    for copy in copies:
        copy.wait()


def body(node_features, weight, out_bias, edge_tiles, tile_column, tile_count, grad_hidden):
    fd, _, rows = node_features.shape
    blocks = lax.axis_size("feat")
    nodes = lax.axis_size("node")
    zs = blocks // 2
    tr = rows // blocks
    hw = weight.shape[1]
    hc = hw // CHUNKS
    slots = edge_tiles.shape[2]
    sizes = (zs, nodes, slots, tr, fd, hw, nodes * rows)
    vmem = pl.BlockSpec(memory_space=pltpu.VMEM)
    hbm = pl.BlockSpec(memory_space=pltpu.HBM)
    dma = pltpu.SemaphoreType.DMA
    c = CHUNKS
    scratch = [
        pltpu.SMEM((1, 1, slots), jnp.int32),
        pltpu.SMEM((1, 1), jnp.int32),
        pltpu.VMEM((fd, hw), BF16),
        pltpu.VMEM((1, hw), F32),
        pltpu.VMEM((slots, tr, tr), BF16),
        pltpu.VMEM((2 * tr, hw), BF16),
        pltpu.VMEM((zs, fd, tr), BF16),
        pltpu.VMEM((zs, 2 * fd, tr), BF16),
        pltpu.VMEM((2 * fd, hw), BF16),
        pltpu.VMEM((2 * tr, 2 * zs * tr), BF16),
        pltpu.VMEM((c, zs - 1, tr, hc), BF16),
        pltpu.VMEM((c, zs - 1, tr, hc), BF16),
        pltpu.VMEM((c, 2 * zs, tr, hc), BF16),
        pltpu.VMEM((c, 2 * tr, hc), BF16),
        pltpu.VMEM((c, zs - 1, tr, hc), BF16),
        pltpu.VMEM((c, zs - 1, tr, hc), BF16),
        pltpu.VMEM((c, 2 * zs, tr, hc), BF16),
        pltpu.VMEM((c, nodes, fd, hc), BF16),
        dma((6,)),
        dma,
        dma,
        dma((12,)),
        dma((4,)),
        dma((zs,)),
        dma((c,)),
        dma((c, zs - 1)),
        dma((c,)),
        dma((c,)),
        dma((c, zs - 1)),
        dma((c,)),
        dma((c,)),
        pltpu.SemaphoreType.REGULAR,
        pltpu.SemaphoreType.REGULAR,
    ]
    hidden, grad_feat, weight_grad = pl.pallas_call(
        functools.partial(kernel, sizes),
        out_shape=(
            pltpu.VMEM((tr, hw), BF16),
            pltpu.VMEM((fd, rows), BF16),
            pltpu.VMEM((fd, hw), F32),
        ),
        in_specs=[hbm] * 7,
        out_specs=(vmem, vmem, vmem),
        scratch_shapes=scratch,
        compiler_params=pltpu.CompilerParams(
            collective_id=0, has_side_effects=True, vmem_limit_bytes=62 * 1024 * 1024
        ),
        name="sage",
    )(
        tile_column,
        tile_count,
        node_features.reshape(fd, rows),
        weight,
        out_bias.reshape(1, hw),
        edge_tiles.reshape(slots, tr, tr),
        grad_hidden.reshape(tr, hw),
    )
    hidden, grad_feat, weight_grad = pl.pallas_call(
        write_out,
        out_shape=(
            jax.ShapeDtypeStruct((tr, hw), BF16),
            jax.ShapeDtypeStruct((fd, rows), BF16),
            jax.ShapeDtypeStruct((fd, hw), F32),
        ),
        in_specs=[vmem] * 3,
        out_specs=(hbm,) * 3,
        scratch_shapes=[dma((3,))],
        name="write_out",
    )(*(pltpu.with_memory_space_constraint(x, pltpu.VMEM)
        for x in (hidden, grad_feat, weight_grad)))
    return (hidden[None], grad_feat[:, None, :], weight_grad)


def solution(mesh):
    return jax.shard_map(
        body,
        mesh=mesh,
        in_specs=(
            P("feat", "node", None),
            P("feat", None),
            P(),
            P("node", "feat", None, None, None),
            P("node", "feat", None),
            P("node", "feat"),
            P("node", "feat", None),
        ),
        out_specs=(P("node", "feat", None), P("feat", "node", None), P("feat", None)),
        check_vma=False,
    )
```

```python
import functools
import math

import jax
import jax.numpy as jnp
from jax import lax
from jax.experimental import pallas as pl
from jax.experimental.pallas import tpu as pltpu
from jax.sharding import PartitionSpec as P

MESH = pl.DeviceIdType.MESH
F32 = jnp.float32
BF16 = jnp.bfloat16
CHUNKS = 2
ROOT = math.sqrt(2.0 / math.pi)


def flip(index, bit):
    return index + bit * (1 - 2 * ((index // bit) % 2))


def flip_many(index, mask, steps):
    for j in range(steps):
        if (mask >> j) & 1:
            index = flip(index, 1 << j)
    return index


def tn(a, b):
    return lax.dot_general(a, b, (((0,), (0,)), ((), ())), preferred_element_type=F32)


def nt(a, b):
    return lax.dot_general(a, b, (((1,), (1,)), ((), ())), preferred_element_type=F32)


def nn(a, b):
    return lax.dot_general(a, b, (((1,), (0,)), ((), ())), preferred_element_type=F32)


def landed(ref, sem):
    pltpu.make_async_copy(ref, ref, sem).wait()


def kernel(sizes, cols_hbm, count_hbm, feats, weight_hbm, bias_hbm, tiles_hbm, grad_hbm,
           hidden, grad_feat, weight_grad,
           cols, count, weight, bias, tiles, grads,
           x_send, x_pair, w_pair, a_full, rs_out, rs_in, gath, sc_full, rt_out, rt_in,
           ggath, wg_in,
           small_s, xa_s, xb_s, sent_s, ex_r, x_r, rs_r, ag_r, fa_r, rt_r, gg_r, fw_r, wg_r,
           far, aside):
    zs, nodes, slots, tr, fd, hw, total = sizes
    zbits, nbits = zs.bit_length() - 1, nodes.bit_length() - 1
    hc = hw // CHUNKS
    ks = range(CHUNKS)
    feat_at = lax.axis_index("feat")
    node_at = lax.axis_index("node")
    core = feat_at % 2
    z = feat_at // 2
    mate = {"feat": z * 2 + 1 - core}
    line = zs == 4
    square = nodes == 4
    inner = jnp.logical_or(z == 1, z == 2)
    outer = jnp.logical_not(inner)

    zrel = [flip_many(z, r, zbits) for r in range(zs)]

    def z_peer(r):
        return {"feat": zrel[r] * 2 + core}

    def n_peer(n):
        return {"node": flip_many(node_at, n, nbits)}

    def push(src, dst, ss, rr, dev):
        pltpu.make_async_remote_copy(
            src_ref=src, dst_ref=dst, send_sem=ss, recv_sem=rr,
            device_id=dev, device_id_type=MESH).start()

    def signal(sem, dev):
        pl.semaphore_signal(sem, inc=1, device_id=dev, device_id_type=MESH)

    barrier = pltpu.get_barrier_semaphore()
    near_n = [1, 2] if square else list(range(1, nodes))
    near_z = [1] if line else list(range(1, zs))
    for r in near_z:
        signal(barrier, z_peer(r))
    if line:
        @pl.when(inner)
        def _():
            signal(barrier, z_peer(3))
    for n in near_n:
        signal(barrier, n_peer(n))
    signal(barrier, mate)

    def rows_of(r, parity):
        return pl.multiple_of((zrel[r] * 2 + parity) * tr, tr)

    def fetch(src, dst, sem):
        copy = pltpu.make_async_copy(src, dst, sem)
        copy.start()
        return copy

    order = list(reversed(range(1, zs)))
    loads = [fetch(src, dst, small_s.at[i]) for i, (src, dst) in enumerate((
        (weight_hbm, weight), (cols_hbm, cols), (count_hbm, count), (tiles_hbm, tiles),
        (bias_hbm, bias), (grad_hbm, grads.at[pl.ds(0, tr)])))]
    for r in range(zs):
        fetch(feats.at[:, pl.ds(rows_of(r, core), tr)], x_pair.at[r, pl.ds(0, fd)], xa_s)
    for r in range(zs):
        fetch(feats.at[:, pl.ds(rows_of(r, 1 - core), tr)], x_send.at[r], xb_s)
    loads[0].wait()
    w_pair[0:fd, :] = weight[...]
    for i in range(1, 4):
        loads[i].wait()
    live = count[0, 0]

    def listed(block):
        where = jnp.int32(0)
        alive = jnp.int32(0)
        for s in range(slots):
            hit = cols[0, 0, s] == block
            where = jnp.where(hit, s, where)
            alive = jnp.where(hit, jnp.where(s < live, 1, 0), alive)
        return tiles[where] * alive.astype(BF16)

    half = zs * tr

    def mask_tiles():
        for p in range(2):
            for r in range(zs):
                parity = core if p == 0 else 1 - core
                at = p * half + r * tr
                a_full[0:tr, at:at + tr] = listed(zrel[r] * 2 + parity)

    landed(x_pair.at[:, pl.ds(0, fd)], xa_s)
    landed(x_send, xb_s)

    greeted = 1 + len(near_n) + len(near_z)
    if line:
        greeted = greeted + jnp.where(inner, 1, 0)
    pl.semaphore_wait(barrier, greeted)
    push(weight, w_pair.at[pl.ds(fd, fd)], sent_s.at[0], ex_r.at[0], mate)
    for r in order + [0]:
        push(x_send.at[r], x_pair.at[r, pl.ds(fd, fd)], sent_s.at[1], x_r.at[r], mate)
    if square:
        signal(aside, n_peer(1))
    if line:
        @pl.when(inner)
        def _():
            signal(far, z_peer(3))
            pl.semaphore_wait(far, 1)
            signal(far, z_peer(1))
    for copy in loads[4:]:
        copy.wait()

    def swap_tiles():
        push(a_full.at[pl.ds(0, tr), pl.ds(0, half)],
             a_full.at[pl.ds(tr, tr), pl.ds(half, half)], sent_s.at[2], ex_r.at[1], mate)
        push(a_full.at[pl.ds(0, tr), pl.ds(half, half)],
             a_full.at[pl.ds(tr, tr), pl.ds(0, half)], sent_s.at[3], ex_r.at[2], mate)
        push(grads.at[pl.ds(0, tr)], grads.at[pl.ds(tr, tr)], sent_s.at[4], ex_r.at[3], mate)

    def hs(k):
        return slice(k * hc, (k + 1) * hc)

    def send_terms(k, make, out, into, ss, rr):
        for r in order:
            out[k, r - 1] = make(k, r).astype(BF16)
            push(out.at[k, r - 1], into.at[k, r - 1], ss, rr.at[k], z_peer(r))
        return make(k, 0)

    def take_terms(k, kept, into, rr):
        landed(into.at[k], rr.at[k])
        for r in order:
            kept = kept + into[k, r - 1].astype(F32)
        return kept.astype(BF16)

    def gather_send(k, buf, ss, rr):
        for r in order:
            push(buf.at[k, 0], buf.at[k, r], ss, rr.at[k, r - 1], z_peer(r))

    def forward(k, r, buf, ss, rr):
        push(buf.at[k, r], buf.at[k, zs + r], ss, rr.at[k], mate)

    def gather_pass(k, buf, rr, ss, ff):
        for r in order:
            landed(buf.at[k, r], rr.at[k, r - 1])
        push(buf.at[k, pl.ds(1, zs - 1)], buf.at[k, pl.ds(zs + 1, zs - 1)], ss, ff.at[k], mate)

    def project(k, r):
        if k == 0:
            landed(x_pair.at[r, pl.ds(fd, fd)], x_r.at[r])
        return tn(x_pair[r], w_pair[:, hs(k)])

    landed(w_pair.at[pl.ds(fd, fd)], ex_r.at[0])
    if line:
        @pl.when(outer)
        def _():
            pl.semaphore_wait(far, 1)
    kept = [send_terms(k, project, rs_out, rs_in, sent_s.at[5], rs_r) for k in ks]
    mask_tiles()
    swap_tiles()
    landed(a_full.at[pl.ds(tr, tr), pl.ds(half, half)], ex_r.at[1])
    landed(a_full.at[pl.ds(tr, tr), pl.ds(0, half)], ex_r.at[2])
    row_scale = lax.rsqrt(jnp.sum(a_full[...].astype(F32), axis=1, keepdims=True))
    landed(grads.at[pl.ds(tr, tr)], ex_r.at[3])
    for k in ks:
        gath[k, 0] = take_terms(k, kept[k], rs_in, rs_r)
        gather_send(k, gath, sent_s.at[6], ag_r)
        forward(k, 0, gath, sent_s.at[7], fa_r)

    def terms(k, r):
        return tn(a_full[:, r * tr:(r + 1) * tr], sc_full[k])

    kept = []
    for k in ks:
        gather_pass(k, gath, ag_r, sent_s.at[7], fa_r)
        summed = nn(a_full[:, 0:half], gath[k, 0:zs].reshape(half, hc))
        landed(gath.at[k, pl.ds(zs, zs)], fa_r.at[k])
        summed = summed + nn(a_full[:, half:], gath[k, zs:].reshape(half, hc))
        v = summed * row_scale + bias[:, hs(k)]
        v2 = v * v
        t = jnp.tanh(ROOT * (v + 0.044715 * v2 * v))
        slope = 0.5 * (1.0 + t) + 0.5 * v * (1.0 - t * t) * (ROOT * (1.0 + 3 * 0.044715 * v2))
        grad_pre = grads[:, hs(k)].astype(F32) * slope
        sc_full[k] = (grad_pre * row_scale).astype(BF16)
        kept.append(send_terms(k, terms, rt_out, rt_in, sent_s.at[8], rt_r))
        hidden[:, hs(k)] = (0.5 * v[0:tr] * (1.0 + t[0:tr])).astype(BF16)

    for k in ks:
        ggath[k, 0] = take_terms(k, kept[k], rt_in, rt_r)
        gather_send(k, ggath, sent_s.at[9], gg_r)
        forward(k, 0, ggath, sent_s.at[10], fw_r)
    scale = 1.0 / math.sqrt(total)

    if square:
        pl.semaphore_wait(aside, 1)
    for k in ks:
        acc = nn(x_pair[0, 0:fd, :], ggath[k, 0])
        for r in order:
            landed(ggath.at[k, r], gg_r.at[k, r - 1])
            forward(k, r, ggath, sent_s.at[10], fw_r)
            acc = acc + nn(x_pair[r, 0:fd, :], ggath[k, r])
        landed(ggath.at[k, pl.ds(zs, zs)], fw_r.at[k])
        for r in range(zs):
            acc = acc + nn(x_send[r], ggath[k, zs + r])
        wg_in[k, 0] = acc.astype(BF16)
        for n in reversed(range(1, nodes)):
            push(wg_in.at[k, 0], wg_in.at[k, n], sent_s.at[11], wg_r.at[k], n_peer(n))
    for r in range(zs):
        for parity, at in ((core, r), (1 - core, zs + r)):
            total_rows = nt(weight[:, hs(0)], ggath[0, at])
            for k in range(1, CHUNKS):
                total_rows = total_rows + nt(weight[:, hs(k)], ggath[k, at])
            grad_feat[:, pl.ds(rows_of(r, parity), tr)] = total_rows.astype(BF16)
    for i, ref in enumerate((
            weight, x_send, a_full.at[pl.ds(0, tr), pl.ds(0, half)],
            a_full.at[pl.ds(0, tr), pl.ds(half, half)], grads.at[pl.ds(0, tr)],
            rs_out, rs_out, gath.at[:, pl.ds(0, zs)], rt_out, rt_out,
            ggath.at[:, pl.ds(0, zs)])):
        landed(ref, sent_s.at[i])
    for k in ks:
        landed(wg_in.at[k, pl.ds(1, nodes - 1)], wg_r.at[k])
        level = [wg_in[k, n].astype(F32) for n in range(nodes)]
        while len(level) > 1:
            level = [level[i] + level[i + 1] for i in range(0, len(level), 2)]
        weight_grad[:, hs(k)] = level[0] * scale
    landed(wg_in.at[:, pl.ds(1, nodes - 1)], sent_s.at[11])


def write_out(a, b, c, a_out, b_out, c_out, sems):
    pairs = ((a, a_out), (b, b_out), (c, c_out))
    copies = [pltpu.make_async_copy(x, y, sems.at[i]) for i, (x, y) in enumerate(pairs)]
    for copy in copies:
        copy.start()
    for copy in copies:
        copy.wait()


def body(node_features, weight, out_bias, edge_tiles, tile_column, tile_count, grad_hidden):
    fd, _, rows = node_features.shape
    blocks = lax.axis_size("feat")
    nodes = lax.axis_size("node")
    zs = blocks // 2
    tr = rows // blocks
    hw = weight.shape[1]
    hc = hw // CHUNKS
    slots = edge_tiles.shape[2]
    sizes = (zs, nodes, slots, tr, fd, hw, nodes * rows)
    vmem = pl.BlockSpec(memory_space=pltpu.VMEM)
    hbm = pl.BlockSpec(memory_space=pltpu.HBM)
    dma = pltpu.SemaphoreType.DMA
    c = CHUNKS
    scratch = [
        pltpu.SMEM((1, 1, slots), jnp.int32),
        pltpu.SMEM((1, 1), jnp.int32),
        pltpu.VMEM((fd, hw), BF16),
        pltpu.VMEM((1, hw), F32),
        pltpu.VMEM((slots, tr, tr), BF16),
        pltpu.VMEM((2 * tr, hw), BF16),
        pltpu.VMEM((zs, fd, tr), BF16),
        pltpu.VMEM((zs, 2 * fd, tr), BF16),
        pltpu.VMEM((2 * fd, hw), BF16),
        pltpu.VMEM((2 * tr, 2 * zs * tr), BF16),
        pltpu.VMEM((c, zs - 1, tr, hc), BF16),
        pltpu.VMEM((c, zs - 1, tr, hc), BF16),
        pltpu.VMEM((c, 2 * zs, tr, hc), BF16),
        pltpu.VMEM((c, 2 * tr, hc), BF16),
        pltpu.VMEM((c, zs - 1, tr, hc), BF16),
        pltpu.VMEM((c, zs - 1, tr, hc), BF16),
        pltpu.VMEM((c, 2 * zs, tr, hc), BF16),
        pltpu.VMEM((c, nodes, fd, hc), BF16),
        dma((6,)),
        dma,
        dma,
        dma((12,)),
        dma((4,)),
        dma((zs,)),
        dma((c,)),
        dma((c, zs - 1)),
        dma((c,)),
        dma((c,)),
        dma((c, zs - 1)),
        dma((c,)),
        dma((c,)),
        pltpu.SemaphoreType.REGULAR,
        pltpu.SemaphoreType.REGULAR,
    ]
    hidden, grad_feat, weight_grad = pl.pallas_call(
        functools.partial(kernel, sizes),
        out_shape=(
            pltpu.VMEM((tr, hw), BF16),
            pltpu.VMEM((fd, rows), BF16),
            pltpu.VMEM((fd, hw), F32),
        ),
        in_specs=[hbm] * 7,
        out_specs=(vmem, vmem, vmem),
        scratch_shapes=scratch,
        compiler_params=pltpu.CompilerParams(
            collective_id=0, has_side_effects=True, vmem_limit_bytes=62 * 1024 * 1024
        ),
        name="sage",
    )(
        tile_column,
        tile_count,
        node_features.reshape(fd, rows),
        weight,
        out_bias.reshape(1, hw),
        edge_tiles.reshape(slots, tr, tr),
        grad_hidden.reshape(tr, hw),
    )
    hidden, grad_feat, weight_grad = pl.pallas_call(
        write_out,
        out_shape=(
            jax.ShapeDtypeStruct((tr, hw), BF16),
            jax.ShapeDtypeStruct((fd, rows), BF16),
            jax.ShapeDtypeStruct((fd, hw), F32),
        ),
        in_specs=[vmem] * 3,
        out_specs=(hbm,) * 3,
        scratch_shapes=[dma((3,))],
        name="write_out",
    )(*(pltpu.with_memory_space_constraint(x, pltpu.VMEM)
        for x in (hidden, grad_feat, weight_grad)))
    return (hidden[None], grad_feat[:, None, :], weight_grad)


def solution(mesh):
    return jax.shard_map(
        body,
        mesh=mesh,
        in_specs=(
            P("feat", "node", None),
            P("feat", None),
            P(),
            P("node", "feat", None, None, None),
            P("node", "feat", None),
            P("node", "feat"),
            P("node", "feat", None),
        ),
        out_specs=(P("node", "feat", None), P("feat", "node", None), P("feat", None)),
        check_vma=False,
    )
```

```python
import functools
import math

import jax
import jax.numpy as jnp
from jax import lax
from jax.experimental import pallas as pl
from jax.experimental.pallas import tpu as pltpu
from jax.sharding import PartitionSpec as P

MESH = pl.DeviceIdType.MESH
F32 = jnp.float32
BF16 = jnp.bfloat16
CHUNKS = 2
ROOT = math.sqrt(2.0 / math.pi)


def flip(index, bit):
    return index + bit * (1 - 2 * ((index // bit) % 2))


def flip_many(index, mask, steps):
    for j in range(steps):
        if (mask >> j) & 1:
            index = flip(index, 1 << j)
    return index


def tn(a, b):
    return lax.dot_general(a, b, (((0,), (0,)), ((), ())), preferred_element_type=F32)


def nt(a, b):
    return lax.dot_general(a, b, (((1,), (1,)), ((), ())), preferred_element_type=F32)


def nn(a, b):
    return lax.dot_general(a, b, (((1,), (0,)), ((), ())), preferred_element_type=F32)


def landed(ref, sem):
    pltpu.make_async_copy(ref, ref, sem).wait()


def kernel(sizes, cols_hbm, count_hbm, feats, weight_hbm, bias_hbm, tiles_hbm, grad_hbm,
           hidden, grad_feat, weight_grad,
           cols, count, weight, bias, tiles, grads,
           x_send, x_pair, w_pair, a_full, rs_out, rs_in, gath, sc_full, rt_out, rt_in,
           ggath, wg_in,
           small_s, xa_s, xb_s, sent_s, ex_r, x_r, rs_r, ag_r, fa_r, rt_r, gg_r, fw_r, wg_r,
           far, aside):
    zs, nodes, slots, tr, fd, hw, total = sizes
    zbits, nbits = zs.bit_length() - 1, nodes.bit_length() - 1
    hc = hw // CHUNKS
    ks = range(CHUNKS)
    feat_at = lax.axis_index("feat")
    node_at = lax.axis_index("node")
    core = feat_at % 2
    z = feat_at // 2
    mate = {"feat": z * 2 + 1 - core}
    line = zs == 4
    square = nodes == 4
    inner = jnp.logical_or(z == 1, z == 2)
    outer = jnp.logical_not(inner)

    zrel = [flip_many(z, r, zbits) for r in range(zs)]

    def z_peer(r):
        return {"feat": zrel[r] * 2 + core}

    def n_peer(n):
        return {"node": flip_many(node_at, n, nbits)}

    def push(src, dst, ss, rr, dev):
        pltpu.make_async_remote_copy(
            src_ref=src, dst_ref=dst, send_sem=ss, recv_sem=rr,
            device_id=dev, device_id_type=MESH).start()

    def signal(sem, dev):
        pl.semaphore_signal(sem, inc=1, device_id=dev, device_id_type=MESH)

    barrier = pltpu.get_barrier_semaphore()
    near_n = [1, 2] if square else list(range(1, nodes))
    near_z = [1] if line else list(range(1, zs))
    for r in near_z:
        signal(barrier, z_peer(r))
    if line:
        @pl.when(inner)
        def _():
            signal(barrier, z_peer(3))
    for n in near_n:
        signal(barrier, n_peer(n))
    signal(barrier, mate)

    def rows_of(r, parity):
        return pl.multiple_of((zrel[r] * 2 + parity) * tr, tr)

    def fetch(src, dst, sem):
        copy = pltpu.make_async_copy(src, dst, sem)
        copy.start()
        return copy

    order = list(reversed(range(1, zs)))
    loads = [fetch(src, dst, small_s.at[i]) for i, (src, dst) in enumerate((
        (weight_hbm, weight), (cols_hbm, cols), (count_hbm, count), (tiles_hbm, tiles),
        (bias_hbm, bias), (grad_hbm, grads.at[pl.ds(0, tr)])))]
    for r in range(zs):
        fetch(feats.at[:, pl.ds(rows_of(r, core), tr)], x_pair.at[r, pl.ds(0, fd)], xa_s)
    for r in range(zs):
        fetch(feats.at[:, pl.ds(rows_of(r, 1 - core), tr)], x_send.at[r], xb_s)
    loads[0].wait()
    w_pair[0:fd, :] = weight[...]
    for i in range(1, 4):
        loads[i].wait()
    live = count[0, 0]

    def listed(block):
        where = jnp.int32(0)
        alive = jnp.int32(0)
        for s in range(slots):
            hit = cols[0, 0, s] == block
            where = jnp.where(hit, s, where)
            alive = jnp.where(hit, jnp.where(s < live, 1, 0), alive)
        return tiles[where] * alive.astype(BF16)

    half = zs * tr

    def mask_tiles():
        for p in range(2):
            for r in range(zs):
                parity = core if p == 0 else 1 - core
                at = p * half + r * tr
                a_full[0:tr, at:at + tr] = listed(zrel[r] * 2 + parity)

    landed(x_pair.at[:, pl.ds(0, fd)], xa_s)
    landed(x_send, xb_s)

    greeted = 1 + len(near_n) + len(near_z)
    if line:
        greeted = greeted + jnp.where(inner, 1, 0)
    pl.semaphore_wait(barrier, greeted)
    push(weight, w_pair.at[pl.ds(fd, fd)], sent_s.at[0], ex_r.at[0], mate)
    for r in order + [0]:
        push(x_send.at[r], x_pair.at[r, pl.ds(fd, fd)], sent_s.at[1], x_r.at[r], mate)
    if square:
        signal(aside, n_peer(1))
    if line:
        @pl.when(inner)
        def _():
            signal(far, z_peer(3))
            pl.semaphore_wait(far, 1)
            signal(far, z_peer(1))
    for copy in loads[4:]:
        copy.wait()

    def swap_tiles():
        push(a_full.at[pl.ds(0, tr), pl.ds(0, half)],
             a_full.at[pl.ds(tr, tr), pl.ds(half, half)], sent_s.at[2], ex_r.at[1], mate)
        push(a_full.at[pl.ds(0, tr), pl.ds(half, half)],
             a_full.at[pl.ds(tr, tr), pl.ds(0, half)], sent_s.at[3], ex_r.at[2], mate)
        push(grads.at[pl.ds(0, tr)], grads.at[pl.ds(tr, tr)], sent_s.at[4], ex_r.at[3], mate)

    def hs(k):
        return slice(k * hc, (k + 1) * hc)

    def send_terms(k, make, out, into, ss, rr):
        for r in order:
            out[k, r - 1] = make(k, r).astype(BF16)
            push(out.at[k, r - 1], into.at[k, r - 1], ss, rr.at[k], z_peer(r))
        return make(k, 0)

    def take_terms(k, kept, into, rr):
        landed(into.at[k], rr.at[k])
        for r in order:
            kept = kept + into[k, r - 1].astype(F32)
        return kept.astype(BF16)

    def gather_send(k, buf, ss, rr):
        for r in order:
            push(buf.at[k, 0], buf.at[k, r], ss, rr.at[k, r - 1], z_peer(r))

    def forward(k, r, buf, ss, rr):
        push(buf.at[k, r], buf.at[k, zs + r], ss, rr.at[k], mate)

    def gather_pass(k, buf, rr, ss, ff):
        landed(buf.at[k, 1], rr.at[k, 0])
        forward(k, 1, buf, ss, ff)
        for r in order[:-1]:
            landed(buf.at[k, r], rr.at[k, r - 1])
        push(buf.at[k, pl.ds(2, zs - 2)], buf.at[k, pl.ds(zs + 2, zs - 2)], ss, ff.at[k], mate)

    def project(k, r):
        if k == 0:
            landed(x_pair.at[r, pl.ds(fd, fd)], x_r.at[r])
        return tn(x_pair[r], w_pair[:, hs(k)])

    landed(w_pair.at[pl.ds(fd, fd)], ex_r.at[0])
    if line:
        @pl.when(outer)
        def _():
            pl.semaphore_wait(far, 1)
    kept = [send_terms(k, project, rs_out, rs_in, sent_s.at[5], rs_r) for k in ks]
    mask_tiles()
    swap_tiles()
    landed(a_full.at[pl.ds(tr, tr), pl.ds(half, half)], ex_r.at[1])
    landed(a_full.at[pl.ds(tr, tr), pl.ds(0, half)], ex_r.at[2])
    row_scale = lax.rsqrt(jnp.sum(a_full[...].astype(F32), axis=1, keepdims=True))
    landed(grads.at[pl.ds(tr, tr)], ex_r.at[3])
    for k in ks:
        gath[k, 0] = take_terms(k, kept[k], rs_in, rs_r)
        gather_send(k, gath, sent_s.at[6], ag_r)
        forward(k, 0, gath, sent_s.at[7], fa_r)

    def terms(k, r):
        return tn(a_full[:, r * tr:(r + 1) * tr], sc_full[k])

    kept = []
    for k in ks:
        gather_pass(k, gath, ag_r, sent_s.at[7], fa_r)
        summed = nn(a_full[:, 0:half], gath[k, 0:zs].reshape(half, hc))
        landed(gath.at[k, pl.ds(zs, zs)], fa_r.at[k])
        summed = summed + nn(a_full[:, half:], gath[k, zs:].reshape(half, hc))
        v = summed * row_scale + bias[:, hs(k)]
        v2 = v * v
        t = jnp.tanh(ROOT * (v + 0.044715 * v2 * v))
        slope = 0.5 * (1.0 + t) + 0.5 * v * (1.0 - t * t) * (ROOT * (1.0 + 3 * 0.044715 * v2))
        grad_pre = grads[:, hs(k)].astype(F32) * slope
        sc_full[k] = (grad_pre * row_scale).astype(BF16)
        kept.append(send_terms(k, terms, rt_out, rt_in, sent_s.at[8], rt_r))
        hidden[:, hs(k)] = (0.5 * v[0:tr] * (1.0 + t[0:tr])).astype(BF16)

    for k in ks:
        ggath[k, 0] = take_terms(k, kept[k], rt_in, rt_r)
        gather_send(k, ggath, sent_s.at[9], gg_r)
        forward(k, 0, ggath, sent_s.at[10], fw_r)
    scale = 1.0 / math.sqrt(total)

    if square:
        pl.semaphore_wait(aside, 1)
    for k in ks:
        acc = nn(x_pair[0, 0:fd, :], ggath[k, 0])
        for r in order:
            landed(ggath.at[k, r], gg_r.at[k, r - 1])
            forward(k, r, ggath, sent_s.at[10], fw_r)
            acc = acc + nn(x_pair[r, 0:fd, :], ggath[k, r])
        landed(ggath.at[k, pl.ds(zs, zs)], fw_r.at[k])
        for r in range(zs):
            acc = acc + nn(x_send[r], ggath[k, zs + r])
        wg_in[k, 0] = acc.astype(BF16)
        for n in reversed(range(1, nodes)):
            push(wg_in.at[k, 0], wg_in.at[k, n], sent_s.at[11], wg_r.at[k], n_peer(n))
    for r in range(zs):
        for parity, at in ((core, r), (1 - core, zs + r)):
            total_rows = nt(weight[:, hs(0)], ggath[0, at])
            for k in range(1, CHUNKS):
                total_rows = total_rows + nt(weight[:, hs(k)], ggath[k, at])
            grad_feat[:, pl.ds(rows_of(r, parity), tr)] = total_rows.astype(BF16)
    for i, ref in enumerate((
            weight, x_send, a_full.at[pl.ds(0, tr), pl.ds(0, half)],
            a_full.at[pl.ds(0, tr), pl.ds(half, half)], grads.at[pl.ds(0, tr)],
            rs_out, rs_out, gath.at[:, pl.ds(0, zs)], rt_out, rt_out,
            ggath.at[:, pl.ds(0, zs)])):
        landed(ref, sent_s.at[i])
    for k in ks:
        landed(wg_in.at[k, pl.ds(1, nodes - 1)], wg_r.at[k])
        level = [wg_in[k, n].astype(F32) for n in range(nodes)]
        while len(level) > 1:
            level = [level[i] + level[i + 1] for i in range(0, len(level), 2)]
        weight_grad[:, hs(k)] = level[0] * scale
    landed(wg_in.at[:, pl.ds(1, nodes - 1)], sent_s.at[11])


def write_out(a, b, c, a_out, b_out, c_out, sems):
    pairs = ((a, a_out), (b, b_out), (c, c_out))
    copies = [pltpu.make_async_copy(x, y, sems.at[i]) for i, (x, y) in enumerate(pairs)]
    for copy in copies:
        copy.start()
    for copy in copies:
        copy.wait()


def body(node_features, weight, out_bias, edge_tiles, tile_column, tile_count, grad_hidden):
    fd, _, rows = node_features.shape
    blocks = lax.axis_size("feat")
    nodes = lax.axis_size("node")
    zs = blocks // 2
    tr = rows // blocks
    hw = weight.shape[1]
    hc = hw // CHUNKS
    slots = edge_tiles.shape[2]
    sizes = (zs, nodes, slots, tr, fd, hw, nodes * rows)
    vmem = pl.BlockSpec(memory_space=pltpu.VMEM)
    hbm = pl.BlockSpec(memory_space=pltpu.HBM)
    dma = pltpu.SemaphoreType.DMA
    c = CHUNKS
    scratch = [
        pltpu.SMEM((1, 1, slots), jnp.int32),
        pltpu.SMEM((1, 1), jnp.int32),
        pltpu.VMEM((fd, hw), BF16),
        pltpu.VMEM((1, hw), F32),
        pltpu.VMEM((slots, tr, tr), BF16),
        pltpu.VMEM((2 * tr, hw), BF16),
        pltpu.VMEM((zs, fd, tr), BF16),
        pltpu.VMEM((zs, 2 * fd, tr), BF16),
        pltpu.VMEM((2 * fd, hw), BF16),
        pltpu.VMEM((2 * tr, 2 * zs * tr), BF16),
        pltpu.VMEM((c, zs - 1, tr, hc), BF16),
        pltpu.VMEM((c, zs - 1, tr, hc), BF16),
        pltpu.VMEM((c, 2 * zs, tr, hc), BF16),
        pltpu.VMEM((c, 2 * tr, hc), BF16),
        pltpu.VMEM((c, zs - 1, tr, hc), BF16),
        pltpu.VMEM((c, zs - 1, tr, hc), BF16),
        pltpu.VMEM((c, 2 * zs, tr, hc), BF16),
        pltpu.VMEM((c, nodes, fd, hc), BF16),
        dma((6,)),
        dma,
        dma,
        dma((12,)),
        dma((4,)),
        dma((zs,)),
        dma((c,)),
        dma((c, zs - 1)),
        dma((c,)),
        dma((c,)),
        dma((c, zs - 1)),
        dma((c,)),
        dma((c,)),
        pltpu.SemaphoreType.REGULAR,
        pltpu.SemaphoreType.REGULAR,
    ]
    hidden, grad_feat, weight_grad = pl.pallas_call(
        functools.partial(kernel, sizes),
        out_shape=(
            pltpu.VMEM((tr, hw), BF16),
            pltpu.VMEM((fd, rows), BF16),
            pltpu.VMEM((fd, hw), F32),
        ),
        in_specs=[hbm] * 7,
        out_specs=(vmem, vmem, vmem),
        scratch_shapes=scratch,
        compiler_params=pltpu.CompilerParams(
            collective_id=0, has_side_effects=True, vmem_limit_bytes=62 * 1024 * 1024
        ),
        name="sage",
    )(
        tile_column,
        tile_count,
        node_features.reshape(fd, rows),
        weight,
        out_bias.reshape(1, hw),
        edge_tiles.reshape(slots, tr, tr),
        grad_hidden.reshape(tr, hw),
    )
    hidden, grad_feat, weight_grad = pl.pallas_call(
        write_out,
        out_shape=(
            jax.ShapeDtypeStruct((tr, hw), BF16),
            jax.ShapeDtypeStruct((fd, rows), BF16),
            jax.ShapeDtypeStruct((fd, hw), F32),
        ),
        in_specs=[vmem] * 3,
        out_specs=(hbm,) * 3,
        scratch_shapes=[dma((3,))],
        name="write_out",
    )(*(pltpu.with_memory_space_constraint(x, pltpu.VMEM)
        for x in (hidden, grad_feat, weight_grad)))
    return (hidden[None], grad_feat[:, None, :], weight_grad)


def solution(mesh):
    return jax.shard_map(
        body,
        mesh=mesh,
        in_specs=(
            P("feat", "node", None),
            P("feat", None),
            P(),
            P("node", "feat", None, None, None),
            P("node", "feat", None),
            P("node", "feat"),
            P("node", "feat", None),
        ),
        out_specs=(P("node", "feat", None), P("feat", "node", None), P("feat", None)),
        check_vma=False,
    )
```
